256 devices in a mesh: sec: 64 (over y, z, core), op: 4 (over x).
Axes of the slice: x: 4, y: 4, z: 8, core: 2. Of those that a mesh axis runs over, the one named last changes fastest.
Arguments:
- wave: bfloat16 [384, 256, 256], P('sec', 'op'), may hold values from -6 to 6
- left_ops: bfloat16 [384, 32, 256, 256], P('sec', 'op'), may hold values from -0.09375 to 0.09375
- right_ops: bfloat16 [384, 32, 256, 256], P('sec', 'op'), may hold values from -0.375 to 0.375
- owner_map: int32 [384, 5], P('sec'), may hold values from 0 to 63, all different within a row; in each aligned block of 6 rows (0 to 5, 6 to 11, ...) at most 2 rows name the same one
- local_map: int32 [384, 5], P('sec'), may hold values from 0 to 5
- op_class: int32 [32], P('op'), may hold values from 0 to 4
Outputs:
- applied: bfloat16 [384, 256, 256], P('sec', 'op')
The draws below stay inside these ranges and needn't reach their ends.
Inputs may be any that keep to these rules, and one draw needn't show every extreme that they name: `owner_map`: each row names 5 different owners; among the rows of one sec index no owner is named more than 2 times, and that count is reached.
All inputs are finite; a program needn't handle non-finite values.
Results may differ from the reference program's by a relative error of at most 0.0049.
Values may be sent and summed in bfloat16 or wider, within the bound.
A program may use at most 128 MiB of HBM per device.

```python
import math
import jax
import jax.numpy as jnp
import numpy as np
from jax import lax

B = 256
NCLS = 5
SEC_DEV = 6
NOPS = 32
SECTORS = 384
CAP = 2
N_SEC = 64


def draw_op_class(key, part):
    order = jax.random.permutation(jax.random.fold_in(key, 11), NOPS).astype(jnp.int32)
    offset = jax.random.randint(jax.random.fold_in(key, 13), (), 0, NCLS).astype(jnp.int32)
    return ((order + offset) % NCLS).astype(jnp.int32)


def place_ends(result, own_key, smallest, top_value):
    place = [jax.random.randint(jax.random.fold_in(own_key, axis), (), 0, length) for axis, length in enumerate(result.shape)]
    main_axis = result.shape.index(max(result.shape))
    neighbour = place[:main_axis] + [(place[main_axis] + 1) % result.shape[main_axis]] + place[main_axis + 1:]
    return result.at[tuple(place)].set(smallest).at[tuple(neighbour)].set(top_value)


def spiked(drawn, stream_key, source, target, parts, factor):
    owner, partner = [(jnp.arange(drawn.shape[dim]) // (drawn.shape[dim] // parts)).reshape([-1 if axis == dim else 1 for axis in range(drawn.ndim)]) for dim in (source, target)]
    chosen = jax.random.permutation(stream_key, parts)[partner]
    strong = (owner == chosen) | (owner == (partner + parts // 2) % parts)
    return jnp.where(strong, factor * drawn, drawn)


def level_of(stream_key, dims, pieces, least, largest):
    level = 1.0
    for dim, shards_of in pieces:
        heights = jax.random.uniform(jax.random.fold_in(jax.random.fold_in(stream_key, 6), dim), (shards_of,), jnp.float32, least / len(pieces), largest / len(pieces))
        level = level * jnp.repeat(jnp.exp(heights), dims[dim] // shards_of).reshape((-1,) + (1,) * (len(dims) - 1 - dim))
    return level


def shared_out(rng, own, number, rows, count, top, limit, slope):
    sequence = jax.random.permutation(rng, count)
    packed, ordinary = load_shares(count, rows * top, limit, slope, True), load_shares(count, rows * top, limit, slope, False)
    places = jnp.arange(count)

    def named(sizes, turn):
        used = int((sizes > 0).sum())
        fixed = max(1, used // 4)
        passed = fixed + (places - fixed + turn * (used - fixed)) % max(1, count - fixed)
        return jnp.zeros((count,), jnp.int32).at[sequence[jnp.where(places < fixed, places, passed)]].set(jnp.asarray(sizes, jnp.int32))

    sizes = jnp.where(number % 4 == 0, named(packed, number // 4), named(ordinary, number - number // 4 - 1))
    mixed = jax.random.permutation(jax.random.fold_in(own, 3), count)
    source_of, sink = mixed[0:count // 2 * 2:2], mixed[1:count // 2 * 2:2]
    slack = jnp.minimum(sizes[source_of] - 1, limit - sizes[sink]) // 2
    slack = jnp.where((source_of == sequence[0]) | (sink == sequence[0]) | (sizes[sink] == 0), 0, jnp.maximum(slack, 0))
    passed = jax.random.randint(jax.random.fold_in(own, 4), (count // 2,), 0, 1 << 20) % (slack + 1)
    sizes = sizes.at[source_of].add(-passed).at[sink].add(passed)
    items = jnp.searchsorted(jnp.cumsum(sizes), jnp.arange(rows * top), side="right").astype(jnp.int32)
    table = items.reshape(top, rows).T
    table = table[jax.random.permutation(jax.random.fold_in(own, 1), rows)]
    turn = jax.random.randint(jax.random.fold_in(own, 2), (rows, 1), 0, top)
    return jnp.take_along_axis(table, (jnp.arange(top)[None, :] + turn) % top, axis=1)


def load_shares(number_of, total, bound, skew, full):
    weights = [(1 << 20) // math.isqrt(standing ** skew) + 1 for standing in range(1, number_of + 1)]
    largest = bound if full else min(bound, max(-(-total // number_of), total * weights[0] // sum(weights)))
    least = 1 if total - largest >= number_of - 1 else 0
    counts, rest = [largest] + [least] * (number_of - 1), total - largest - least * (number_of - 1)
    while rest > 0:
        candidates = [i for i in range(1, number_of) if counts[i] < largest] or [i for i in range(1, number_of) if counts[i] < bound]
        pool, left = sum([weights[i] for i in candidates]), rest
        for i in candidates:
            extra = min(bound - counts[i], max(1, left * weights[i] // pool), rest)
            counts[i] = counts[i] + extra
            rest = rest - extra
    return np.array(counts)


def bell_draw(own_key, dims, spread, most, shards=(), kind=jnp.bfloat16):
    result = jax.random.normal(own_key, dims, jnp.float32) * spread
    if len(shards) > 0:
        result = level_of(own_key, dims, shards, -0.22, 0.18) * result
    return jnp.clip(result, min=-most, max=most).astype(kind)


def heavy_noise(rng, shape, spread, limit, shards, heavy, held_as=jnp.bfloat16):
    drawn = spread * jax.random.normal(rng, shape, jnp.float32)
    if shards:
        drawn = drawn * level_of(rng, shape, shards, -0.22, 0.18)
    return jnp.clip(spiked(drawn, jax.random.fold_in(rng, 3), *heavy), -limit, limit).astype(held_as)


def setup_inputs(seed: int = 0) -> dict:
    splits = jax.random.split(jax.random.key(seed), 7)
    wave = bell_draw(splits[0], (SECTORS, B, B), 1.0, 6.0, ((0, 64), (1, 4)))
    left_ops = heavy_noise(splits[1], (SECTORS, NOPS, B, B), (B * NOPS) ** -0.5, 0.09375, ((0, 64), (1, 4)), (1, 2, 4, 2.0))
    right_ops = bell_draw(splits[2], (SECTORS, NOPS, B, B), B ** -0.5, 0.375, ((0, 64), (1, 4)))
    owner_map_keys = jax.random.split(jax.random.fold_in(splits[3], 1), SECTORS // SEC_DEV)
    owner_map_turns = jax.random.permutation(jax.random.fold_in(splits[3], 3), SECTORS // SEC_DEV)
    owner_map = jax.vmap(lambda own, number: shared_out(jax.random.fold_in(splits[3], 2), own, number, SEC_DEV, N_SEC, NCLS, CAP, 2))(owner_map_keys, owner_map_turns).reshape((SECTORS, NCLS))
    local_map = place_ends(jax.random.randint(splits[4], (SECTORS, NCLS), 0, SEC_DEV), jax.random.fold_in(splits[4], 1), 0, SEC_DEV - 1).astype(jnp.int32)
    op_class = draw_op_class(jax.random.fold_in(splits[6], 71), 0)
    return dict(wave=wave, left_ops=left_ops, right_ops=right_ops, owner_map=owner_map, local_map=local_map, op_class=op_class)


def reference(wave, left_ops, right_ops, owner_map, local_map, op_class):
    source = (owner_map[:, op_class] * SEC_DEV + local_map[:, op_class]).astype(jnp.int32)

    def per_target(target_args):
        left_blocks, right_blocks, picked = target_args
        blocks = wave[picked].astype(jnp.float32)
        lifted = jnp.einsum('onk,okm->onm', left_blocks.astype(jnp.float32), blocks).astype(jnp.bfloat16)
        lifted = lax.optimization_barrier(lifted)
        summed = jnp.einsum('onm,okm->nk', lifted.astype(jnp.float32), right_blocks.astype(jnp.float32))
        return summed.astype(jnp.bfloat16)

    return lax.map(per_target, (left_ops, right_ops, source))
```

```python
import jax
import jax.numpy as jnp
from jax import lax
from jax.sharding import PartitionSpec as P


def shards(wave, left_ops, right_ops, owner_map, local_map, op_class):
    sec_size = lax.axis_size("sec")
    sec_dev, classes = owner_map.shape
    block_size = left_ops.shape[2]
    request_count = sec_dev * classes
    capacity = max(2, (request_count + sec_size - 1) // sec_size + 1)
    owners = owner_map.reshape(request_count)
    local_rows = local_map.reshape(request_count)
    devices = jnp.arange(sec_size, dtype=jnp.int32)
    onehot = (owners[:, None] == devices[None, :]).astype(jnp.int32)
    before = jnp.cumsum(onehot, axis=0) - onehot
    ranks_in = jnp.sum(before * onehot, axis=1)
    slot_of = owners * capacity + ranks_in
    request_table = jnp.full((sec_size * capacity,), -1, jnp.int32).at[slot_of].set(local_rows)
    wanted = lax.all_to_all(
        request_table.reshape(sec_size, capacity), "sec", split_axis=0, concat_axis=0, tiled=True
    )
    block_index = jnp.maximum(wanted, 0).reshape(sec_size * capacity)
    rows = wave.shape[1]
    outgoing = wave[block_index].reshape(sec_size, capacity, rows, block_size)
    fetched = lax.all_to_all(outgoing, "sec", split_axis=0, concat_axis=0, tiled=True)
    fetched = fetched.reshape(sec_size * capacity, rows, block_size)
    compact = fetched[slot_of]
    sources = lax.all_gather(compact, "op", axis=1, tiled=True)
    sources = sources.reshape(sec_dev, classes, block_size, block_size)
    chosen = sources[:, op_class]
    lifted = jnp.einsum(
        "tonk,tokm->tonm", left_ops, chosen, preferred_element_type=jnp.float32
    ).astype(jnp.bfloat16)
    partial_value = jnp.einsum(
        "tonm,tokm->tnk", lifted, right_ops, preferred_element_type=jnp.float32
    )
    return lax.psum_scatter(partial_value, "op", scatter_dimension=1, tiled=True).astype(
        jnp.bfloat16
    )


def solution(mesh):
    in_specs = (
        P("sec", "op", None),
        P("sec", "op", None, None),
        P("sec", "op", None, None),
        P("sec", None),
        P("sec", None),
        P("op"),
    )
    out_specs = P("sec", "op", None)
    return jax.shard_map(shards, mesh=mesh, in_specs=in_specs, out_specs=out_specs, check_vma=False)
```

```python
import jax
import jax.numpy as jnp
from jax import lax
from jax.sharding import PartitionSpec as P


def shards(wave, left_ops, right_ops, owner_map, local_map, op_class):
    sec_dev, classes = owner_map.shape
    block_size = left_ops.shape[2]
    source = owner_map * sec_dev + local_map
    every_wave = lax.all_gather(wave, "sec", axis=0, tiled=True)
    compact = every_wave[source.reshape(sec_dev * classes)]
    sources = lax.all_gather(compact, "op", axis=1, tiled=True)
    sources = sources.reshape(sec_dev, classes, block_size, block_size)
    chosen = sources[:, op_class]
    lifted = jnp.einsum(
        "tonk,tokm->tonm", left_ops, chosen, preferred_element_type=jnp.float32
    ).astype(jnp.bfloat16)
    partial_value = jnp.einsum(
        "tonm,tokm->tnk", lifted, right_ops, preferred_element_type=jnp.float32
    )
    return lax.psum_scatter(partial_value, "op", scatter_dimension=1, tiled=True).astype(
        jnp.bfloat16
    )


def solution(mesh):
    in_specs = (
        P("sec", "op", None),
        P("sec", "op", None, None),
        P("sec", "op", None, None),
        P("sec", None),
        P("sec", None),
        P("op"),
    )
    out_specs = P("sec", "op", None)
    return jax.shard_map(shards, mesh=mesh, in_specs=in_specs, out_specs=out_specs, check_vma=False)
```

```python
import jax
import jax.numpy as jnp
from jax import lax
from jax.sharding import PartitionSpec as P


def shards(wave, left_ops, right_ops, owner_map, local_map, op_class):
    sec_dev, classes = owner_map.shape
    block_size = left_ops.shape[2]
    source = owner_map * sec_dev + local_map
    every_wave = lax.all_gather(wave, "sec", axis=0, tiled=True)
    compact = every_wave[source.reshape(sec_dev * classes)]
    sources = lax.all_gather(compact, "op", axis=1, tiled=True)
    sources = sources.reshape(sec_dev, classes, block_size, block_size)
    chosen = sources[:, op_class]
    lifted = jnp.einsum(
        "tonk,tokm->tonm", left_ops, chosen, preferred_element_type=jnp.float32
    ).astype(jnp.bfloat16)
    partial_value = jnp.einsum(
        "tonm,tokm->tnk", lifted, right_ops, preferred_element_type=jnp.float32
    ).astype(jnp.bfloat16)
    return lax.psum_scatter(partial_value, "op", scatter_dimension=1, tiled=True)


def solution(mesh):
    in_specs = (
        P("sec", "op", None),
        P("sec", "op", None, None),
        P("sec", "op", None, None),
        P("sec", None),
        P("sec", None),
        P("op"),
    )
    out_specs = P("sec", "op", None)
    return jax.shard_map(shards, mesh=mesh, in_specs=in_specs, out_specs=out_specs, check_vma=False)
```
